256 devices in a mesh: bead: 32 (over y, z), space: 8 (over x, core).
Axes of the slice: x: 4, y: 4, z: 8, core: 2. Of those that a mesh axis runs over, the one named last changes fastest.
Arguments:
- positions: float32 [32, 3, 131072], P('bead', None, 'space'), may hold values from -5.5 to 5.5
- charges: float32 [131072], P('space'), may hold values from -1 to 1
- polarizability: float32 [131072], P('space'), may hold values from 0.03 to 0.12
- masses: float32 [131072], P('space'), may hold values from 1 to 16
- neighbors: int32 [1024, 8], P('space'), may hold values from 0 to 135, as said below
Outputs:
- forces: float32 [32, 3, 131072], P('bead', None, 'space')
- dipoles: float32 [3, 131072], P(None, ('space', 'bead'))
The draws below stay inside these ranges and needn't reach their ends.
Inputs may be any that keep to these rules, and one draw needn't show every extreme that they name: `neighbors`: row t lists 8 different tiles by their index in its domain's extended numbering: the last 4 tiles of the previous domain, the domain's own 128 tiles, the first 4 tiles of the next domain (domains form a cycle). Every listed tile lies within 4 tiles of tile t, and the two tiles at distance exactly 4 on either side are always listed.
All inputs are finite; a program needn't handle non-finite values.
Results may differ from the reference program's by a relative error of at most 0.0001.
Values sent between devices are 32-bit elements; how exact they have to be, the bound alone decides.
No kernel may reach another device: no remote copies, remote signals or barrier semaphores. Data moves between devices by JAX's collectives and lax.ppermute only.
A program may use at most 64 MiB of HBM per device.

```python
import math
import jax
import jax.numpy as jnp
from jax import lax

TILE = 128
NBR = 8
HALO_T = 4
ITERS = 3
ATOM_DEV = 16384
BEADS = 32
ATOMS = 131072
TILE_DEV = 128
TILES_ALL = 1024


def draw_positions(key, part):
    base_key = jax.random.fold_in(key, 11)
    bead_key = jax.random.fold_in(key, 12)
    base = jnp.clip(jax.random.normal(base_key, (1, 3, ATOMS), jnp.float32), -4.0, 4.0)
    spread = jnp.clip(0.3 * jax.random.normal(bead_key, (BEADS, 3, ATOMS), jnp.float32), -1.5, 1.5)
    return base + spread


def draw_neighbors(key, part):
    inner_count = 2 * HALO_T - 1
    scores = jax.random.randint(jax.random.fold_in(key, 21), (TILES_ALL, inner_count), 0, 1 << 20)
    scores = scores * inner_count + jnp.arange(inner_count, dtype=jnp.int32)[None, :]
    ranking = jnp.argsort(scores, axis=1).astype(jnp.int32)
    chosen = ranking[:, :NBR - 2] - (HALO_T - 1)
    extremes = jnp.broadcast_to(jnp.array([-HALO_T, HALO_T], jnp.int32), (TILES_ALL, 2))
    offsets = jnp.concatenate([extremes[:, :1], chosen, extremes[:, 1:]], axis=1)
    local_tile = (jnp.arange(TILES_ALL, dtype=jnp.int32) % TILE_DEV)[:, None]
    return (local_tile + HALO_T + offsets).astype(jnp.int32)


def block_levels(key, shape, split, low, largest):
    loudness = 1.0
    for axis_at, parts in split:
        steps = jax.random.uniform(jax.random.fold_in(jax.random.fold_in(key, 6), axis_at), (parts,), jnp.float32, low / len(split), largest / len(split))
        loudness = loudness * jnp.repeat(jnp.exp(steps), shape[axis_at] // parts).reshape((-1,) + (1,) * (len(shape) - 1 - axis_at))
    return loudness


def setup_inputs(seed: int = 0) -> dict:
    key_list = jax.random.split(jax.random.key(seed), 6)
    positions = draw_positions(jax.random.fold_in(key_list[5], 71), 0)
    charges = jnp.clip(jax.random.uniform(key_list[1], (ATOMS,), jnp.float32, -1.0, 1.0) * block_levels(key_list[1], (ATOMS,), ((0, 8),), -0.4, 0.0), -1.0, 1.0)
    polarizability = jnp.clip(jnp.exp(math.log(0.12) - 1.3862944 * jax.random.uniform(key_list[2], (ATOMS,), jnp.float32) ** block_levels(key_list[2], (ATOMS,), ((0, 8),), -0.2, 0.2)), 0.03, 0.12)
    masses = jnp.clip(jnp.exp(math.log(16.0) - 2.7725887 * jax.random.uniform(key_list[3], (ATOMS,), jnp.float32) ** block_levels(key_list[3], (ATOMS,), ((0, 8),), -0.2, 0.2)), 1.0, 16.0)
    neighbors = draw_neighbors(jax.random.fold_in(key_list[5], 71), 0)
    return dict(positions=positions, charges=charges, polarizability=polarizability, masses=masses, neighbors=neighbors)


REPULSION = 0.2
SPRING = 0.1


def repulsion_kernel(targets, sources):
    displace = targets[:, :, :, None] - sources[:, :, None, :]
    weight = jnp.exp(-0.5 * jnp.sum(displace * displace, axis=0))
    return REPULSION * jnp.sum(weight[None] * displace, axis=3)


def charge_kernel(targets, sources, charge):
    displace = targets[:, :, :, None] - sources[:, :, None, :]
    weight = jnp.exp(-0.25 * jnp.sum(displace * displace, axis=0)) * charge[0][:, None, :]
    return jnp.sum(weight[None] * displace, axis=3)


def dipole_kernel(targets, sources, dipole):
    displace = targets[:, :, :, None] - sources[:, :, None, :]
    weight = jnp.exp(-0.25 * jnp.sum(displace * displace, axis=0))
    spread_dip = dipole[:, :, None, :]
    projected = jnp.sum(displace * spread_dip, axis=0)
    return jnp.sum(weight[None] * (0.25 * displace * projected[None] - 0.5 * spread_dip), axis=3)


def grouped(kernel, targets, sources):
    tile_count = targets.shape[1]
    group_size = math.gcd(tile_count, 4)

    def split_tiles(tensor):
        return jnp.moveaxis(tensor.reshape(tensor.shape[0], tile_count // group_size, group_size, tensor.shape[2]), 1, 0)

    pieces = tuple(split_tiles(tensor) for tensor in (targets,) + tuple(sources))
    result = lax.map(lambda member: kernel(*member), pieces)
    return jnp.moveaxis(result, 0, 1).reshape(3, tile_count, targets.shape[2])


def tile_table(neighbors):
    tile_total = neighbors.shape[0]
    tiles_domain = ATOM_DEV // TILE
    tile_rows = jnp.arange(tile_total, dtype=jnp.int32)
    domain_start = (tile_rows // tiles_domain) * tiles_domain
    return ((domain_start[:, None] + neighbors - HALO_T) % tile_total).astype(jnp.int32)


def gather_tiles(field, tile_map):
    channels = field.shape[0]
    tiles = field.reshape(channels, tile_map.shape[0], TILE)
    picked = jnp.take(tiles, tile_map, axis=1)
    return picked.reshape(channels, tile_map.shape[0], tile_map.shape[1] * TILE)


def reference(positions, charges, polarizability, masses, neighbors):
    tile_map = tile_table(neighbors)
    tile_total = tile_map.shape[0]

    def bead_forces(coords):
        targets = coords.reshape(3, tile_total, TILE)
        sources = gather_tiles(coords, tile_map)
        return grouped(repulsion_kernel, targets, (sources,)).reshape(3, ATOMS)

    short_range = lax.map(bead_forces, positions)
    cycle_sum = jnp.roll(positions, 1, axis=0) + jnp.roll(positions, -1, axis=0) - 2.0 * positions
    spring = SPRING * masses[None, None, :] * cycle_sum
    centroid = jnp.sum(positions, axis=0) / BEADS
    cent_tiles = centroid.reshape(3, tile_total, TILE)
    cent_sources = gather_tiles(centroid, tile_map)
    charge_sources = gather_tiles(charges[None], tile_map)
    permanent = grouped(charge_kernel, cent_tiles, (cent_sources, charge_sources)).reshape(3, ATOMS)

    def induced(dipole_now):
        return grouped(dipole_kernel, cent_tiles, (cent_sources, gather_tiles(dipole_now, tile_map))).reshape(3, ATOMS)

    dipoles = polarizability[None] * permanent
    for sweep_index in range(ITERS):
        dipoles = polarizability[None] * (permanent + induced(dipoles))
    pulled = charges[None] * induced(dipoles)
    forces = short_range + spring + pulled[None]
    return forces, dipoles
```

```python
import functools
import math

import jax
import jax.numpy as jnp
from jax import lax
from jax.experimental import pallas as pl
from jax.experimental.pallas import tpu as pltpu
from jax.sharding import PartitionSpec as P

TILE = 128
NBR = 8
HALO_T = 4
ITERS = 3
LOG2E = 1.4426950408889634
REPULSION = 0.2
SPRING = 0.1
UNROLL = 4
PLAN = (32, 12, 12, 12, 12, 12, 36)
VMEM = pltpu.MemorySpace.VMEM
SMEM = pltpu.MemorySpace.SMEM


def cols(at, n=TILE):
    return pl.ds(pl.multiple_of(at * TILE, TILE), n)


def split3(x):
    hi = x.astype(jnp.bfloat16).astype(jnp.float32)
    rest = x - hi
    mid = rest.astype(jnp.bfloat16).astype(jnp.float32)
    return hi, mid, rest - mid


def short_kernel(tiles, first, nb_ref, ext_ref, after_ref, out_ref, src, tgt, acc):
    width = src.shape[1]
    x = ext_ref[:, first * TILE : first * TILE + width]
    hi, mid, low = split3(x)
    src[...] = jnp.concatenate([hi, mid, low, hi, mid, hi], 0).astype(jnp.bfloat16)
    row = lax.broadcasted_iota(jnp.int32, hi.shape, 0)
    xyz = row < 3
    hi_t = jnp.where(xyz, hi, jnp.where(row == 3, 1.0, 0.0))
    mid_t = jnp.where(xyz, mid, 0.0)
    low_t = jnp.where(xyz, low, 0.0)
    tgt[...] = jnp.concatenate([hi_t, hi_t, hi_t, mid_t, mid_t, low_t], 0).astype(jnp.bfloat16)

    def finish(n, slot):
        sums = [
            jnp.sum(jnp.transpose(acc[slot, c]), axis=0, keepdims=True) for c in range(4)
        ]
        own = ext_ref[:, cols(n + first + HALO_T)]
        fade = (REPULSION / math.sqrt(LOG2E)) * jnp.exp2(own[3:4])
        pull = jnp.concatenate([sums[1], sums[2], sums[3]], 0)
        out_ref[:, cols(n)] = fade * (own[:3] * sums[0] - pull)

    def body(step, carry):
        for s in range(UNROLL):
            finish(jnp.maximum((step - 1) * UNROLL, 0) + s, s)
        for s in range(UNROLL):
            n = step * UNROLL + s
            lhs = tgt[:, cols(n + HALO_T)]
            at = [nb_ref[n + first, k] - first for k in range(NBR)]
            rows = [
                [
                    jnp.broadcast_to(ext_ref[c : c + 1, cols(at[k] + first)], (8, TILE))
                    for c in range(3)
                ]
                for k in range(NBR)
            ]
            expo = []
            for k in range(0, NBR, 2):
                rhs = jnp.concatenate([src[:, cols(at[k])], src[:, cols(at[k + 1])]], 1)
                expo.append(
                    lax.dot_general(
                        lhs, rhs, (((0,), (0,)), ((), ())), preferred_element_type=jnp.float32
                    )
                )
            for g in range(0, TILE, 8):
                total = None
                for k in range(NBR):
                    half = (k % 2) * TILE
                    u = jnp.exp2(expo[k // 2][g : g + 8, half : half + TILE])
                    parts = [u, u * rows[k][0], u * rows[k][1], u * rows[k][2]]
                    total = parts if k == 0 else [a + b for a, b in zip(total, parts)]
                for c in range(4):
                    acc[s, c, g : g + 8, :] = total[c]
        return carry

    steps = tiles // UNROLL
    for s in range(UNROLL):
        for c in range(4):
            acc[s, c] = jnp.zeros((TILE, TILE), jnp.float32)
    lax.fori_loop(0, steps, body, 0)
    for s in range(UNROLL):
        finish((steps - 1) * UNROLL + s, s)


def short_range(ext8, neighbors, first, tiles, after):
    width = (tiles + 2 * HALO_T) * TILE
    pairs = tiles * TILE * NBR * TILE
    return pl.pallas_call(
        functools.partial(short_kernel, tiles, first),
        out_shape=jax.ShapeDtypeStruct((3, tiles * TILE), jnp.float32),
        in_specs=[
            pl.BlockSpec(memory_space=SMEM),
            pl.BlockSpec(memory_space=VMEM),
            pl.BlockSpec(memory_space=pl.ANY),
        ],
        out_specs=pl.BlockSpec(memory_space=VMEM),
        scratch_shapes=[
            pltpu.VMEM((48, width), jnp.bfloat16),
            pltpu.VMEM((48, width), jnp.bfloat16),
            pltpu.VMEM((UNROLL, 4, TILE, TILE), jnp.float32),
        ],
        cost_estimate=pl.CostEstimate(
            flops=pairs * 100, bytes_accessed=4 * 11 * width, transcendentals=pairs
        ),
        compiler_params=pltpu.CompilerParams(vmem_limit_bytes=16 << 20),
        name="short_range",
    )(neighbors, ext8, after)


def centre_kernel(mode, own_tiles, nb_ref, *refs):
    ins, (out_ref, win, spread, acc) = refs, refs[-4:]
    size = own_tiles * TILE
    if mode == "permanent":
        before, own, after, charge, alpha = ins[:5]
    else:
        before, own, after, dip_b, dip_o, dip_a, scale = ins[:7]
    parts = (before, own, after)
    for p in range(3):
        win[0:3, p * size : (p + 1) * size] = parts[p][...]
    if mode == "permanent":
        win[3:4, :] = charge[...]
    else:
        for p, dip in enumerate((dip_b, dip_o, dip_a)):
            win[3:6, p * size : (p + 1) * size] = dip[0:3, :]

    def body(t):
        for c in range(3):
            line = win[c : c + 1, (t + HALO_T) * TILE : (t + HALO_T + 1) * TILE]
            spread[t, c] = jnp.transpose(jnp.broadcast_to(line, (TILE, TILE)))
        at = [nb_ref[t, k] for k in range(NBR)]
        wide = 4 if mode == "permanent" else 6
        rows = [
            [jnp.broadcast_to(win[c : c + 1, cols(at[k])], (8, TILE)) for c in range(wide)]
            for k in range(NBR)
        ]
        for g in range(0, TILE, 8):
            me = [spread[t, c, g : g + 8, :] for c in range(3)]
            total = None
            for k in range(NBR):
                d = [me[c] - rows[k][c] for c in range(3)]
                r2 = d[0] * d[0] + d[1] * d[1] + d[2] * d[2]
                w = jnp.exp2((-0.25 * LOG2E) * r2)
                if mode == "permanent":
                    w = w * rows[k][3]
                    add = [w * d[c] for c in range(3)]
                else:
                    m = rows[k][3:6]
                    p = 0.25 * (d[0] * m[0] + d[1] * m[1] + d[2] * m[2])
                    add = [w * (p * d[c] - 0.5 * m[c]) for c in range(3)]
                total = add if k == 0 else [a + b for a, b in zip(total, add)]
            for c in range(3):
                acc[t, c, g : g + 8, :] = total[c]
        here = slice(t * TILE, (t + 1) * TILE)
        for c in range(3):
            s = jnp.sum(jnp.transpose(acc[t, c]), axis=0, keepdims=True)
            if mode == "permanent":
                out_ref[c : c + 1, here] = alpha[:, here] * s
                out_ref[3 + c : 4 + c, here] = s
            elif mode == "dipole":
                out_ref[c : c + 1, here] = scale[:, here] * (ins[7][3 + c : 4 + c, here] + s)
            else:
                line = scale[:, here] * s
                out_ref[:, c : c + 1, here] = jnp.broadcast_to(line, (out_ref.shape[0], 1, TILE))

    for t in range(own_tiles):
        body(t)


def centre(mode, copies, after, nb, *arrays):
    size = arrays[0].shape[1]
    shape = {"permanent": (6, size), "dipole": (3, size), "pulled": (copies, 3, size)}[mode]
    pairs = size * NBR * TILE
    return pl.pallas_call(
        functools.partial(centre_kernel, mode, size // TILE),
        out_shape=jax.ShapeDtypeStruct(shape, jnp.float32),
        in_specs=[pl.BlockSpec(memory_space=SMEM)]
        + [pl.BlockSpec(memory_space=VMEM)] * len(arrays)
        + [pl.BlockSpec(memory_space=pl.ANY)] * len(after),
        out_specs=pl.BlockSpec(memory_space=VMEM),
        scratch_shapes=[
            pltpu.VMEM((8, 3 * size), jnp.float32),
            pltpu.VMEM((HALO_T, 3, TILE, TILE), jnp.float32),
            pltpu.VMEM((HALO_T, 3, TILE, TILE), jnp.float32),
        ],
        cost_estimate=pl.CostEstimate(
            flops=pairs * 100, bytes_accessed=4 * 24 * size, transcendentals=pairs
        ),
        compiler_params=pltpu.CompilerParams(vmem_limit_bytes=16 << 20),
    )(nb, *arrays, *after)


def pack_kernel(order, pos_ref, out_ref):
    size = out_ref.shape[2]
    for b, share in enumerate(order):
        out_ref[b] = pos_ref[:, share * size : (share + 1) * size]


def pack(order, coords):
    size = coords.shape[1] // len(order)
    return pl.pallas_call(
        functools.partial(pack_kernel, order),
        out_shape=jax.ShapeDtypeStruct((len(order), 3, size), jnp.float32),
        in_specs=[pl.BlockSpec(memory_space=VMEM)],
        out_specs=pl.BlockSpec(memory_space=VMEM),
        compiler_params=pltpu.CompilerParams(vmem_limit_bytes=8 << 20),
        name="pack",
    )(coords)


def total_kernel(order, plan, pos, last, following, masses, every, *refs):
    short, out_ref = refs[:-1], refs[-1]
    size = every.shape[2]
    for b, share in enumerate(order):
        here = slice(share * size, (share + 1) * size)
        at, piece = share * size // TILE, 0
        while at >= plan[piece]:
            at, piece = at - plan[piece], piece + 1
        spring = (SPRING * masses[:, here]) * (
            last[:, here] + following[:, here] - 2.0 * pos[:, here]
        )
        force = short[piece][:, at * TILE : at * TILE + size] + spring + every[b]
        for c in range(3):
            out_ref[c, :, here] = force[c : c + 1]


def total(order, plan, *arrays):
    width = arrays[0].shape[1]
    return pl.pallas_call(
        functools.partial(total_kernel, order, plan),
        out_shape=jax.ShapeDtypeStruct((3, 1, width), jnp.float32),
        in_specs=[pl.BlockSpec(memory_space=VMEM)] * len(arrays),
        out_specs=pl.BlockSpec(memory_space=VMEM),
        compiler_params=pltpu.CompilerParams(vmem_limit_bytes=8 << 20),
        name="total",
    )(*arrays)


def per_device(beads, spaces, positions, charges, polarizability, masses, neighbors):
    coords = positions[0]
    atom_dev = coords.shape[1]
    rim = HALO_T * TILE
    size = atom_dev // beads
    own_tiles = size // TILE
    assert size == rim
    across = math.gcd(beads, 8)
    bead = lax.axis_index("bead")

    def share_of(b):
        row, at = b // across, b % across
        return row * across + (across - 1 - at if row % 2 else at)

    order = [share_of(b) for b in range(beads)]
    row, at = bead // across, bead % across
    share = row * across + jnp.where(row % 2 == 1, across - 1 - at, at)
    start = share * size

    def place(g):
        return share_of(g % beads) * spaces + g // beads

    count = beads * spaces
    fore = [(place(g), place((g + 1) % count)) for g in range(count)]
    back = [(j, i) for i, j in fore]
    both = ("bead", "space")

    def around(x):
        return lax.ppermute(x, both, fore), x, lax.ppermute(x, both, back)

    up = [(s, (s + 1) % spaces) for s in range(spaces)]
    down = [(j, i) for i, j in up]
    held = jnp.concatenate([coords, charges[None]], 0)
    before = lax.ppermute(held[:, atom_dev - rim :], "space", up)
    after = lax.ppermute(held[:, :rim], "space", down)
    ext = jnp.concatenate([before, held, after], 1)
    x = ext[:3] * math.sqrt(LOG2E)
    ext8 = jnp.concatenate(
        [x, -0.5 * jnp.sum(x * x, 0, keepdims=True), jnp.zeros((4, x.shape[1]), x.dtype)], 0
    )
    near_charge = lax.dynamic_slice(ext[3:4], (0, start), (1, size + 2 * rim))

    shares = pack(order, coords)
    cent = jnp.sum(lax.all_to_all(shares, "bead", 0, 0), axis=0) / beads

    own_rows = lax.dynamic_slice(neighbors, (share * own_tiles, 0), (own_tiles, NBR))
    nb = own_rows - share * own_tiles
    alpha = lax.dynamic_slice(polarizability, (start,), (size,))[None]
    charge = lax.dynamic_slice(charges, (start,), (size,))[None]

    tiles = atom_dev // TILE
    plan = [n * tiles // sum(PLAN) for n in PLAN]
    short = []

    def fill(after):
        first = sum(plan[: len(short)])
        short.append(short_range(ext8, neighbors, first, plan[len(short)], after))
        return short[-1]

    wait = fill(shares)
    cent, wait = lax.optimization_barrier((cent, wait))
    c3 = around(cent)
    wait = fill(cent)
    state = centre("permanent", beads, (wait,), nb, *c3, near_charge, alpha)

    turn = [(b, (b + 1) % beads) for b in range(beads)]
    turn_back = [(j, i) for i, j in turn]
    late, state = lax.optimization_barrier((coords, state))
    last = lax.ppermute(late, "bead", turn)
    following = lax.ppermute(late, "bead", turn_back)
    dip = state[:3]
    for sweep in range(ITERS):
        d3 = around(dip)
        hold = (fill(dip), last, following) if sweep == 1 else (fill(dip),)
        dip = centre("dipole", beads, hold, nb, *c3, *d3, alpha, state)
    d3 = around(dip)
    pulled = centre("pulled", beads, (fill(dip),), nb, *c3, *d3, charge)
    fill(pulled)
    every = lax.all_to_all(pulled, "bead", 0, 0)
    forces = total(order, plan, coords, last, following, masses[None], every, *short)
    forces = forces.transpose(1, 0, 2)
    dipoles = lax.ppermute(dip, "bead", [(b, share_of(b)) for b in range(beads)])
    return forces, dipoles


def solution(mesh):
    in_specs = (P("bead", None, "space"), P("space"), P("space"), P("space"), P("space", None))
    out_specs = (P("bead", None, "space"), P(None, ("space", "bead")))

    def body(*arrays):
        return per_device(mesh.shape["bead"], mesh.shape["space"], *arrays)

    return jax.shard_map(
        body, mesh=mesh, in_specs=in_specs, out_specs=out_specs, check_vma=False
    )
```

```python
import functools
import math

import jax
import jax.numpy as jnp
from jax import lax
from jax.experimental import pallas as pl
from jax.experimental.pallas import tpu as pltpu
from jax.sharding import PartitionSpec as P

TILE = 128
NBR = 8
HALO_T = 4
ITERS = 3
LOG2E = 1.4426950408889634
REPULSION = 0.2
SPRING = 0.1
UNROLL = 4
PLAN = (28, 12, 16, 12, 16, 12, 32)
VMEM = pltpu.MemorySpace.VMEM
SMEM = pltpu.MemorySpace.SMEM


def cols(at, n=TILE):
    return pl.ds(pl.multiple_of(at * TILE, TILE), n)


def split3(x):
    hi = x.astype(jnp.bfloat16).astype(jnp.float32)
    rest = x - hi
    mid = rest.astype(jnp.bfloat16).astype(jnp.float32)
    return hi, mid, rest - mid


def short_kernel(tiles, first, nb_ref, ext_ref, after_ref, out_ref, src, tgt, acc, expo):
    width = src.shape[1]
    x = ext_ref[:, first * TILE : first * TILE + width]
    hi, mid, low = split3(x)
    src[...] = jnp.concatenate([hi, mid, low, hi, mid, hi], 0).astype(jnp.bfloat16)
    row = lax.broadcasted_iota(jnp.int32, hi.shape, 0)
    xyz = row < 3
    hi_t = jnp.where(xyz, hi, jnp.where(row == 3, 1.0, 0.0))
    mid_t = jnp.where(xyz, mid, 0.0)
    low_t = jnp.where(xyz, low, 0.0)
    own = slice(HALO_T * TILE, (HALO_T + tiles) * TILE)
    both = jnp.concatenate([hi_t, hi_t, hi_t, mid_t, mid_t, low_t], 0)[:, own]
    tgt[...] = jnp.transpose(both.astype(jnp.bfloat16))

    def finish(n, slot):
        sums = [
            jnp.sum(jnp.transpose(acc[slot, c]), axis=0, keepdims=True) for c in range(4)
        ]
        own = ext_ref[:, cols(n + first + HALO_T)]
        fade = (REPULSION / math.sqrt(LOG2E)) * jnp.exp2(own[3:4])
        pull = jnp.concatenate([sums[1], sums[2], sums[3]], 0)
        out_ref[:, cols(n)] = fade * (own[:3] * sums[0] - pull)

    def sources(n):
        return [nb_ref[n + first, k] - first for k in range(NBR)]

    def exponents(n, at):
        lhs = tgt[cols(n), :]
        both = [
            jnp.concatenate([src[:, cols(at[k])], src[:, cols(at[k + 1])]], 1)
            for k in range(0, NBR, 2)
        ]
        return [
            jnp.dot(lhs, rhs, preferred_element_type=jnp.float32)
            for rhs in both
        ]

    def prepare(n):
        for k, part in enumerate(exponents(n, sources(n))):
            expo[:, 2 * k * TILE : 2 * (k + 1) * TILE] = part

    def body(step, carry):
        for s in range(UNROLL // 2, UNROLL):
            finish(jnp.maximum((step - 1) * UNROLL, 0) + s, s)
        for s in range(UNROLL):
            if s == UNROLL // 2:
                for done in range(s):
                    finish(step * UNROLL + done, done)
            n = step * UNROLL + s
            at = sources(n)
            rows = [
                [
                    jnp.broadcast_to(ext_ref[c : c + 1, cols(at[k] + first)], (8, TILE))
                    for c in range(3)
                ]
                for k in range(NBR)
            ]
            parts = None if s == 0 else exponents(n, at)
            for g in range(0, TILE, 8):
                total = None
                for k in range(NBR):
                    half = (k % 2) * TILE
                    if s == 0:
                        e = expo[g : g + 8, k * TILE : (k + 1) * TILE]
                    else:
                        e = parts[k // 2][g : g + 8, half : half + TILE]
                    u = jnp.exp2(e)
                    add = [u, u * rows[k][0], u * rows[k][1], u * rows[k][2]]
                    total = add if k == 0 else [a + b for a, b in zip(total, add)]
                for c in range(4):
                    acc[s, c, g : g + 8, :] = total[c]
        prepare(jnp.minimum((step + 1) * UNROLL, tiles - 1))
        return carry

    steps = tiles // UNROLL
    for s in range(UNROLL):
        for c in range(4):
            acc[s, c] = jnp.zeros((TILE, TILE), jnp.float32)
    prepare(0)
    lax.fori_loop(0, steps, body, 0)
    for s in range(UNROLL // 2, UNROLL):
        finish((steps - 1) * UNROLL + s, s)


def short_range(ext8, neighbors, first, tiles, after):
    width = (tiles + 2 * HALO_T) * TILE
    pairs = tiles * TILE * NBR * TILE
    return pl.pallas_call(
        functools.partial(short_kernel, tiles, first),
        out_shape=jax.ShapeDtypeStruct((3, tiles * TILE), jnp.float32),
        in_specs=[
            pl.BlockSpec(memory_space=SMEM),
            pl.BlockSpec(memory_space=VMEM),
            pl.BlockSpec(memory_space=pl.ANY),
        ],
        out_specs=pl.BlockSpec(memory_space=VMEM),
        scratch_shapes=[
            pltpu.VMEM((48, width), jnp.bfloat16),
            pltpu.VMEM((tiles * TILE, 48), jnp.bfloat16),
            pltpu.VMEM((UNROLL, 4, TILE, TILE), jnp.float32),
            pltpu.VMEM((TILE, NBR * TILE), jnp.float32),
        ],
        cost_estimate=pl.CostEstimate(
            flops=pairs * 100, bytes_accessed=4 * 11 * width, transcendentals=pairs
        ),
        compiler_params=pltpu.CompilerParams(vmem_limit_bytes=16 << 20),
        name="short_range",
    )(neighbors, ext8, after)


def centre_kernel(mode, own_tiles, nb_ref, *refs):
    ins, (out_ref, win, spread, acc) = refs, refs[-4:]
    size = own_tiles * TILE
    if mode == "permanent":
        before, own, after, charge, alpha = ins[:5]
    else:
        before, own, after, dip_b, dip_o, dip_a, scale = ins[:7]
    parts = (before, own, after)
    for p in range(3):
        win[0:3, p * size : (p + 1) * size] = parts[p][...]
    if mode == "permanent":
        win[3:4, :] = charge[...]
    else:
        for p, dip in enumerate((dip_b, dip_o, dip_a)):
            win[3:6, p * size : (p + 1) * size] = dip[0:3, :]

    def body(t):
        for c in range(3):
            line = win[c : c + 1, (t + HALO_T) * TILE : (t + HALO_T + 1) * TILE]
            spread[t, c] = jnp.transpose(jnp.broadcast_to(line, (TILE, TILE)))
        at = [nb_ref[t, k] for k in range(NBR)]
        wide = 4 if mode == "permanent" else 6
        rows = [
            [jnp.broadcast_to(win[c : c + 1, cols(at[k])], (8, TILE)) for c in range(wide)]
            for k in range(NBR)
        ]
        for g in range(0, TILE, 8):
            me = [spread[t, c, g : g + 8, :] for c in range(3)]
            total = None
            for k in range(NBR):
                d = [me[c] - rows[k][c] for c in range(3)]
                r2 = d[0] * d[0] + d[1] * d[1] + d[2] * d[2]
                w = jnp.exp2((-0.25 * LOG2E) * r2)
                if mode == "permanent":
                    w = w * rows[k][3]
                    add = [w * d[c] for c in range(3)]
                else:
                    m = rows[k][3:6]
                    p = 0.25 * (d[0] * m[0] + d[1] * m[1] + d[2] * m[2])
                    add = [w * (p * d[c] - 0.5 * m[c]) for c in range(3)]
                total = add if k == 0 else [a + b for a, b in zip(total, add)]
            for c in range(3):
                acc[t, c, g : g + 8, :] = total[c]
        here = slice(t * TILE, (t + 1) * TILE)
        for c in range(3):
            s = jnp.sum(jnp.transpose(acc[t, c]), axis=0, keepdims=True)
            if mode == "permanent":
                out_ref[c : c + 1, here] = alpha[:, here] * s
                out_ref[3 + c : 4 + c, here] = s
            elif mode == "dipole":
                out_ref[c : c + 1, here] = scale[:, here] * (ins[7][3 + c : 4 + c, here] + s)
            else:
                line = scale[:, here] * s
                out_ref[:, c : c + 1, here] = jnp.broadcast_to(line, (out_ref.shape[0], 1, TILE))

    for t in range(own_tiles):
        body(t)


def centre(mode, copies, after, nb, *arrays):
    size = arrays[0].shape[1]
    shape = {"permanent": (6, size), "dipole": (3, size), "pulled": (copies, 3, size)}[mode]
    pairs = size * NBR * TILE
    return pl.pallas_call(
        functools.partial(centre_kernel, mode, size // TILE),
        out_shape=jax.ShapeDtypeStruct(shape, jnp.float32),
        in_specs=[pl.BlockSpec(memory_space=SMEM)]
        + [pl.BlockSpec(memory_space=VMEM)] * len(arrays)
        + [pl.BlockSpec(memory_space=pl.ANY)] * len(after),
        out_specs=pl.BlockSpec(memory_space=VMEM),
        scratch_shapes=[
            pltpu.VMEM((8, 3 * size), jnp.float32),
            pltpu.VMEM((HALO_T, 3, TILE, TILE), jnp.float32),
            pltpu.VMEM((HALO_T, 3, TILE, TILE), jnp.float32),
        ],
        cost_estimate=pl.CostEstimate(
            flops=pairs * 100, bytes_accessed=4 * 24 * size, transcendentals=pairs
        ),
        compiler_params=pltpu.CompilerParams(vmem_limit_bytes=16 << 20),
    )(nb, *arrays, *after)


def seat(order, odd, share):
    there = order[len(order) - 1 - share]
    return order[share] + odd * (there - order[share])


def pack_kernel(order, odd_ref, pos_ref, charge_ref, out_ref, first_ref, last_ref):
    size, rim, width = out_ref.shape[2], first_ref.shape[1], pos_ref.shape[2]
    for share in range(len(order)):
        b = seat(order, odd_ref[0], share)
        for c in range(3):
            out_ref[b, c : c + 1, :] = pos_ref[c, :, share * size : (share + 1) * size]
    for ref, low in ((first_ref, 0), (last_ref, width - rim)):
        for c in range(3):
            ref[c : c + 1, :] = pos_ref[c, :, low : low + rim]
        ref[3:4, :] = charge_ref[:, low : low + rim]


def pack(order, rim, odd, coords, charges):
    size = coords.shape[2] // len(order)
    shapes = ((len(order), 3, size), (4, rim), (4, rim))
    return pl.pallas_call(
        functools.partial(pack_kernel, order),
        out_shape=[jax.ShapeDtypeStruct(shape, jnp.float32) for shape in shapes],
        in_specs=[pl.BlockSpec(memory_space=SMEM)] + [pl.BlockSpec(memory_space=VMEM)] * 2,
        out_specs=[pl.BlockSpec(memory_space=VMEM)] * 3,
        compiler_params=pltpu.CompilerParams(vmem_limit_bytes=8 << 20),
        name="pack",
    )(odd, coords, charges)


def extend_kernel(pos_ref, before_ref, after_ref, out_ref):
    rim, width = before_ref.shape[1], pos_ref.shape[2]
    out_ref[4:8, :] = jnp.zeros((4, width + 2 * rim), jnp.float32)
    for at, size, rows in (
        (0, rim, [before_ref[c : c + 1, :] for c in range(3)]),
        (rim, width, [pos_ref[c] for c in range(3)]),
        (rim + width, rim, [after_ref[c : c + 1, :] for c in range(3)]),
    ):
        rows = [math.sqrt(LOG2E) * x for x in rows]
        for c in range(3):
            out_ref[c : c + 1, at : at + size] = rows[c]
        norm = rows[0] * rows[0] + rows[1] * rows[1] + rows[2] * rows[2]
        out_ref[3:4, at : at + size] = -0.5 * norm


def extend(pos, before, after):
    width = pos.shape[2] + 2 * before.shape[1]
    return pl.pallas_call(
        extend_kernel,
        out_shape=jax.ShapeDtypeStruct((8, width), jnp.float32),
        in_specs=[pl.BlockSpec(memory_space=VMEM)] * 3,
        out_specs=pl.BlockSpec(memory_space=VMEM),
        compiler_params=pltpu.CompilerParams(vmem_limit_bytes=8 << 20),
        name="extend",
    )(pos, before, after)


def total_kernel(order, plan, odd_ref, pos, last, following, masses, every, dip, *refs):
    short, (out_ref, dip_ref) = refs[:-2], refs[-2:]
    size = every.shape[2]
    dip_ref[...] = dip[...]
    for share in range(len(order)):
        here = slice(share * size, (share + 1) * size)
        at, piece = share * size // TILE, 0
        while at >= plan[piece]:
            at, piece = at - plan[piece], piece + 1
        weight = SPRING * masses[:, here]
        other = short[piece][:, at * TILE : at * TILE + size] + every[seat(order, odd_ref[0], share)]
        for c in range(3):
            pull = last[c, :, here] + following[c, :, here] - 2.0 * pos[c, :, here]
            out_ref[c, :, here] = other[c : c + 1] + weight * pull


def total(order, plan, odd, *arrays):
    shapes = (arrays[0].shape, arrays[5].shape)
    return pl.pallas_call(
        functools.partial(total_kernel, order, plan),
        out_shape=[jax.ShapeDtypeStruct(shape, jnp.float32) for shape in shapes],
        in_specs=[pl.BlockSpec(memory_space=SMEM)]
        + [pl.BlockSpec(memory_space=VMEM)] * len(arrays),
        out_specs=[pl.BlockSpec(memory_space=VMEM)] * 2,
        compiler_params=pltpu.CompilerParams(vmem_limit_bytes=8 << 20),
        name="total",
    )(odd, *arrays)


def per_device(beads, spaces, positions, charges, polarizability, masses, neighbors):
    coords = positions.transpose(1, 0, 2)
    atom_dev = coords.shape[2]
    rim = HALO_T * TILE
    size = atom_dev // beads
    own_tiles = size // TILE
    assert size == rim
    across = math.gcd(beads, 8)
    bead = lax.axis_index("bead")

    def fold(b):
        row, at = b // across, b % across
        return row * across + (across - 1 - at if row % 2 else at)

    order = [fold(b) for b in range(beads)]
    row, at = bead // across, bead % across
    share = row * across + jnp.where(row % 2 == 1, across - 1 - at, at)
    odd = lax.axis_index("space") % 2
    share = jnp.where(odd == 1, beads - 1 - share, share)
    odd = odd.astype(jnp.int32).reshape(1)
    start = share * size

    def place(g):
        domain = g // beads
        return seat(order, domain % 2, g % beads) * spaces + domain

    count = beads * spaces
    fore = [(place(g), place((g + 1) % count)) for g in range(count)]
    back = [(j, i) for i, j in fore]
    home = [(place(g), (g % beads) * spaces + g // beads) for g in range(count)]
    both = ("bead", "space")

    def around(x):
        return lax.ppermute(x, both, fore), x, lax.ppermute(x, both, back)

    up = [(s, (s + 1) % spaces) for s in range(spaces)]
    down = [(j, i) for i, j in up]
    charges = charges[None]
    shares, first, final = pack(order, rim, odd, coords, charges)
    before = lax.ppermute(final, "space", up)
    after = lax.ppermute(first, "space", down)
    ext8 = extend(coords, before, after)
    near = jnp.concatenate([before[3:], charges, after[3:]], 1)
    near_charge = lax.dynamic_slice(near, (0, start), (1, size + 2 * rim))

    cent = jnp.sum(lax.all_to_all(shares, "bead", 0, 0), axis=0) / beads

    own_rows = lax.dynamic_slice(neighbors, (share * own_tiles, 0), (own_tiles, NBR))
    nb = own_rows - share * own_tiles
    alpha = lax.dynamic_slice(polarizability, (start,), (size,))[None]
    charge = lax.dynamic_slice(charges, (0, start), (1, size))

    tiles = atom_dev // TILE
    plan = [n * tiles // sum(PLAN) for n in PLAN]
    short = []

    def fill(after):
        first = sum(plan[: len(short)])
        short.append(short_range(ext8, neighbors, first, plan[len(short)], after))
        return short[-1]

    wait = fill(shares)
    cent, wait = lax.optimization_barrier((cent, wait))
    c3 = around(cent)
    wait = fill(cent)
    state = centre("permanent", beads, (wait,), nb, *c3, near_charge, alpha)

    turn = [(b, (b + 1) % beads) for b in range(beads)]
    turn_back = [(j, i) for i, j in turn]
    late, state = lax.optimization_barrier((coords, state))
    last = lax.ppermute(late, "bead", turn)
    following = lax.ppermute(late, "bead", turn_back)
    dip = state[:3]
    for sweep in range(ITERS):
        d3 = around(dip)
        hold = (fill(dip), last, following) if sweep == 1 else (fill(dip),)
        dip = centre("dipole", beads, hold, nb, *c3, *d3, alpha, state)
    d3 = around(dip)
    dipoles = lax.ppermute(dip, both, home)
    pulled = centre("pulled", beads, (fill(dip), dipoles), nb, *c3, *d3, charge)
    fill(pulled)
    every = lax.all_to_all(pulled, "bead", 0, 0)
    forces, dipoles = total(
        order, plan, odd, coords, last, following, masses[None], every, dipoles, *short
    )
    return forces.transpose(1, 0, 2), dipoles


def solution(mesh):
    in_specs = (P("bead", None, "space"), P("space"), P("space"), P("space"), P("space", None))
    out_specs = (P("bead", None, "space"), P(None, ("space", "bead")))

    def body(*arrays):
        return per_device(mesh.shape["bead"], mesh.shape["space"], *arrays)

    return jax.shard_map(
        body, mesh=mesh, in_specs=in_specs, out_specs=out_specs, check_vma=False
    )
```

```python
import functools
import math

import jax
import jax.numpy as jnp
from jax import lax
from jax.experimental import pallas as pl
from jax.experimental.pallas import tpu as pltpu
from jax.sharding import PartitionSpec as P

TILE = 128
NBR = 8
HALO_T = 4
ITERS = 3
LOG2E = 1.4426950408889634
REPULSION = 0.2
SPRING = 0.1
UNROLL = 4
PLAN = (36, 16, 16, 16, 16, 16, 12)
VMEM = pltpu.MemorySpace.VMEM
SMEM = pltpu.MemorySpace.SMEM


def cols(at, n=TILE):
    return pl.ds(pl.multiple_of(at * TILE, TILE), n)


def split3(x):
    hi = x.astype(jnp.bfloat16).astype(jnp.float32)
    rest = x - hi
    mid = rest.astype(jnp.bfloat16).astype(jnp.float32)
    return hi, mid, rest - mid


def short_kernel(tiles, first, nb_ref, ext_ref, after_ref, out_ref, src, tgt, acc, expo):
    width = src.shape[1]
    x = ext_ref[:, first * TILE : first * TILE + width]
    hi, mid, low = split3(x)
    src[...] = jnp.concatenate([hi, mid, low, hi, mid, hi], 0).astype(jnp.bfloat16)
    row = lax.broadcasted_iota(jnp.int32, hi.shape, 0)
    xyz = row < 3
    hi_t = jnp.where(xyz, hi, jnp.where(row == 3, 1.0, 0.0))
    mid_t = jnp.where(xyz, mid, 0.0)
    low_t = jnp.where(xyz, low, 0.0)
    own = slice(HALO_T * TILE, (HALO_T + tiles) * TILE)
    both = jnp.concatenate([hi_t, hi_t, hi_t, mid_t, mid_t, low_t], 0)[:, own]
    tgt[...] = jnp.transpose(both.astype(jnp.bfloat16))

    def finish(n, slot):
        sums = [
            jnp.sum(jnp.transpose(acc[slot, c]), axis=0, keepdims=True) for c in range(4)
        ]
        own = ext_ref[:, cols(n + first + HALO_T)]
        fade = (REPULSION / math.sqrt(LOG2E)) * jnp.exp2(own[3:4])
        pull = jnp.concatenate([sums[1], sums[2], sums[3]], 0)
        out_ref[:, cols(n)] = fade * (own[:3] * sums[0] - pull)

    def sources(n):
        return [nb_ref[k, n + first] - first for k in range(NBR)]

    def exponents(n, at):
        lhs = tgt[cols(n), :]
        both = [
            jnp.concatenate([src[:, cols(at[k])], src[:, cols(at[k + 1])]], 1)
            for k in range(0, NBR, 2)
        ]
        return [
            jnp.dot(lhs, rhs, preferred_element_type=jnp.float32)
            for rhs in both
        ]

    def prepare(n):
        for k, part in enumerate(exponents(n, sources(n))):
            expo[:, 2 * k * TILE : 2 * (k + 1) * TILE] = part

    def body(step, carry):
        for s in range(UNROLL // 2, UNROLL):
            finish(jnp.maximum((step - 1) * UNROLL, 0) + s, s)
        for s in range(UNROLL):
            if s == UNROLL // 2:
                for done in range(s):
                    finish(step * UNROLL + done, done)
            n = step * UNROLL + s
            at = sources(n)
            rows = [
                [
                    jnp.broadcast_to(ext_ref[c : c + 1, cols(at[k] + first)], (8, TILE))
                    for c in range(3)
                ]
                for k in range(NBR)
            ]
            parts = None if s == 0 else exponents(n, at)
            for g in range(0, TILE, 8):
                total = None
                for k in range(NBR):
                    half = (k % 2) * TILE
                    if s == 0:
                        e = expo[g : g + 8, k * TILE : (k + 1) * TILE]
                    else:
                        e = parts[k // 2][g : g + 8, half : half + TILE]
                    u = jnp.exp2(e)
                    add = [u, u * rows[k][0], u * rows[k][1], u * rows[k][2]]
                    total = add if k == 0 else [a + b for a, b in zip(total, add)]
                for c in range(4):
                    acc[s, c, g : g + 8, :] = total[c]
        prepare(jnp.minimum((step + 1) * UNROLL, tiles - 1))
        return carry

    steps = tiles // UNROLL
    prepare(0)
    lax.fori_loop(0, steps, body, 0)
    for s in range(UNROLL // 2, UNROLL):
        finish((steps - 1) * UNROLL + s, s)


def short_range(ext8, neighbors, first, tiles, after):
    width = (tiles + 2 * HALO_T) * TILE
    pairs = tiles * TILE * NBR * TILE
    return pl.pallas_call(
        functools.partial(short_kernel, tiles, first),
        out_shape=jax.ShapeDtypeStruct((3, tiles * TILE), jnp.float32),
        in_specs=[
            pl.BlockSpec(memory_space=SMEM),
            pl.BlockSpec(memory_space=VMEM),
            pl.BlockSpec(memory_space=pl.ANY),
        ],
        out_specs=pl.BlockSpec(memory_space=VMEM),
        scratch_shapes=[
            pltpu.VMEM((48, width), jnp.bfloat16),
            pltpu.VMEM((tiles * TILE, 48), jnp.bfloat16),
            pltpu.VMEM((UNROLL, 4, TILE, TILE), jnp.float32),
            pltpu.VMEM((TILE, NBR * TILE), jnp.float32),
        ],
        cost_estimate=pl.CostEstimate(
            flops=pairs * 100, bytes_accessed=4 * 11 * width, transcendentals=pairs
        ),
        compiler_params=pltpu.CompilerParams(vmem_limit_bytes=16 << 20),
        name="short_range",
    )(neighbors, ext8, after)


def rows16(x):
    hi, mid, low = split3(x)
    return jnp.concatenate([hi, mid, low], 0).astype(jnp.bfloat16)


def contract(high, rest, feats):
    dims = (((1,), (1,)), ((), ()))
    out = lax.dot_general(high, feats, dims, preferred_element_type=jnp.float32)
    out += lax.dot_general(rest, feats, dims, preferred_element_type=jnp.float32)
    out = jnp.transpose(out)
    return out[:16] + out[16:32] + out[32:48]


def gather(ref, nb_ref, t):
    return jnp.concatenate([ref[:, cols(nb_ref[t, k])] for k in range(NBR)], 1)


def fade_of(x):
    return jnp.exp2((-0.25 * LOG2E) * jnp.sum(x * x, axis=0, keepdims=True))


def first_kernel(own_tiles, nb_ref, before, own, after, charge, alpha, *refs):
    out_ref, high_ref, rest_ref, win, src, tgt, feats = refs[-7:]
    size = own_tiles * TILE
    for p, part in enumerate((before, own, after)):
        win[0:3, p * size : (p + 1) * size] = part[...]
    x = win[0:3, :]
    q = charge[...]
    y = math.sqrt(0.5 * LOG2E) * x
    norm = -0.5 * jnp.sum(y * y, axis=0, keepdims=True)
    zero = jnp.zeros((4, 3 * size), jnp.float32)
    hi, mid, low = split3(jnp.concatenate([y, norm, zero], 0))
    src[...] = jnp.concatenate([hi, mid, low, hi, mid, hi], 0).astype(jnp.bfloat16)
    row = lax.broadcasted_iota(jnp.int32, hi.shape, 0)
    hi_t = jnp.where(row < 3, hi, jnp.where(row == 3, 1.0, 0.0))
    mid_t, low_t = jnp.where(row < 3, mid, 0.0), jnp.where(row < 3, low, 0.0)
    both = jnp.concatenate([hi_t, hi_t, hi_t, mid_t, mid_t, low_t], 0)[:, size : 2 * size]
    tgt[...] = jnp.transpose(both.astype(jnp.bfloat16))
    feats[...] = rows16(jnp.concatenate([q, q * x, zero, zero, zero], 0))
    for t in range(own_tiles):
        here = slice(t * TILE, (t + 1) * TILE)
        e = jnp.dot(tgt[here, :], gather(src, nb_ref, t), preferred_element_type=jnp.float32)
        u = jnp.exp2(e)
        high = u.astype(jnp.bfloat16)
        rest = (u - high.astype(jnp.float32)).astype(jnp.bfloat16)
        high_ref[here, :] = high
        rest_ref[here, :] = rest
        sums = contract(high, rest, gather(feats, nb_ref, t))
        me = own[:, here]
        field = fade_of(me) * (me * sums[0:1] - sums[1:4])
        out_ref[0:3, here] = alpha[:, here] * field
        out_ref[3:6, here] = field


def next_kernel(last, own_tiles, nb_ref, before, own, after, dip_b, dip_o, dip_a, *refs):
    scale, state, high_ref, rest_ref = refs[:4]
    out_ref, feats = refs[-2:]
    size = own_tiles * TILE
    parts = ((before, dip_b), (own, dip_o), (after, dip_a))
    for p, (place, dip) in enumerate(parts):
        x, m = place[...], dip[0:3, :]
        along = jnp.sum(x * m, axis=0, keepdims=True)
        rows = [m, along, x[0:1] * m, x[1:2] * m, x[2:3] * m, x * along]
        feats[:, p * size : (p + 1) * size] = rows16(jnp.concatenate(rows, 0))
    for t in range(own_tiles):
        here = slice(t * TILE, (t + 1) * TILE)
        sums = contract(high_ref[here, :], rest_ref[here, :], gather(feats, nb_ref, t))
        me = own[:, here]
        ahead = jnp.sum(me * sums[0:3], axis=0, keepdims=True) - sums[3:4]
        turned = [
            jnp.sum(me * sums[4 + 3 * c : 7 + 3 * c], axis=0, keepdims=True) for c in range(3)
        ]
        pull = me * ahead - jnp.concatenate(turned, 0) + sums[13:16]
        field = fade_of(me) * (0.25 * pull - 0.5 * sums[0:3])
        if last:
            line = scale[:, here] * field
            out_ref[:, :, here] = jnp.broadcast_to(line[None], (out_ref.shape[0], 3, TILE))
        else:
            out_ref[:, here] = scale[:, here] * (state[3:6, here] + field)


def centre_call(body, shapes, scratch, nb, arrays, after):
    size = arrays[0].shape[1]
    pairs = size * NBR * TILE
    return pl.pallas_call(
        functools.partial(body, size // TILE),
        out_shape=shapes,
        in_specs=[pl.BlockSpec(memory_space=SMEM)]
        + [pl.BlockSpec(memory_space=VMEM)] * len(arrays)
        + [pl.BlockSpec(memory_space=pl.ANY)] * len(after),
        out_specs=[pl.BlockSpec(memory_space=VMEM)] * len(shapes),
        scratch_shapes=scratch,
        cost_estimate=pl.CostEstimate(
            flops=pairs * 100, bytes_accessed=4 * 24 * size, transcendentals=pairs
        ),
        compiler_params=pltpu.CompilerParams(vmem_limit_bytes=12 << 20),
    )(nb, *arrays, *after)


def centre_first(nb, after, *arrays):
    size = arrays[0].shape[1]
    shapes = [
        jax.ShapeDtypeStruct((6, size), jnp.float32),
        jax.ShapeDtypeStruct((size, NBR * TILE), jnp.bfloat16),
        jax.ShapeDtypeStruct((size, NBR * TILE), jnp.bfloat16),
    ]
    scratch = [
        pltpu.VMEM((8, 3 * size), jnp.float32),
        pltpu.VMEM((48, 3 * size), jnp.bfloat16),
        pltpu.VMEM((size, 48), jnp.bfloat16),
        pltpu.VMEM((48, 3 * size), jnp.bfloat16),
    ]
    return centre_call(first_kernel, shapes, scratch, nb, arrays, after)


def centre_next(copies, nb, after, *arrays):
    size = arrays[0].shape[1]
    shape = (copies, 3, size) if copies else (3, size)
    scratch = [pltpu.VMEM((48, 3 * size), jnp.bfloat16)]
    body = functools.partial(next_kernel, copies > 0)
    shapes = [jax.ShapeDtypeStruct(shape, jnp.float32)]
    return centre_call(body, shapes, scratch, nb, arrays, after)[0]


def seat(order, odd, share):
    there = order[len(order) - 1 - share]
    return order[share] + odd * (there - order[share])


def pack_kernel(order, odd_ref, pos_ref, charge_ref, out_ref, first_ref, last_ref):
    size, rim, width = out_ref.shape[2], first_ref.shape[1], pos_ref.shape[2]
    for share in range(len(order)):
        b = seat(order, odd_ref[0], share)
        for c in range(3):
            out_ref[b, c : c + 1, :] = pos_ref[c, :, share * size : (share + 1) * size]
    for ref, low in ((first_ref, 0), (last_ref, width - rim)):
        for c in range(3):
            ref[c : c + 1, :] = pos_ref[c, :, low : low + rim]
        ref[3:4, :] = charge_ref[:, low : low + rim]


def pack(order, rim, odd, coords, charges):
    size = coords.shape[2] // len(order)
    shapes = ((len(order), 3, size), (4, rim), (4, rim))
    return pl.pallas_call(
        functools.partial(pack_kernel, order),
        out_shape=[jax.ShapeDtypeStruct(shape, jnp.float32) for shape in shapes],
        in_specs=[pl.BlockSpec(memory_space=SMEM)] + [pl.BlockSpec(memory_space=VMEM)] * 2,
        out_specs=[pl.BlockSpec(memory_space=VMEM)] * 3,
        compiler_params=pltpu.CompilerParams(vmem_limit_bytes=8 << 20),
        name="pack",
    )(odd, coords, charges)


def extend_kernel(pos_ref, before_ref, after_ref, out_ref):
    rim, width = before_ref.shape[1], pos_ref.shape[2]
    out_ref[4:8, :] = jnp.zeros((4, width + 2 * rim), jnp.float32)
    for at, size, rows in (
        (0, rim, [before_ref[c : c + 1, :] for c in range(3)]),
        (rim, width, [pos_ref[c] for c in range(3)]),
        (rim + width, rim, [after_ref[c : c + 1, :] for c in range(3)]),
    ):
        rows = [math.sqrt(LOG2E) * x for x in rows]
        for c in range(3):
            out_ref[c : c + 1, at : at + size] = rows[c]
        norm = rows[0] * rows[0] + rows[1] * rows[1] + rows[2] * rows[2]
        out_ref[3:4, at : at + size] = -0.5 * norm


def extend(pos, before, after):
    width = pos.shape[2] + 2 * before.shape[1]
    return pl.pallas_call(
        extend_kernel,
        out_shape=jax.ShapeDtypeStruct((8, width), jnp.float32),
        in_specs=[pl.BlockSpec(memory_space=VMEM)] * 3,
        out_specs=pl.BlockSpec(memory_space=VMEM),
        compiler_params=pltpu.CompilerParams(vmem_limit_bytes=8 << 20),
        name="extend",
    )(pos, before, after)


def total_kernel(order, plan, odd_ref, pos, last, following, masses, every, dip, *refs):
    short, (out_ref, dip_ref) = refs[:-2], refs[-2:]
    size = every.shape[2]
    dip_ref[...] = dip[...]
    for share in range(len(order)):
        here = slice(share * size, (share + 1) * size)
        at, piece = share * size // TILE, 0
        while at >= plan[piece]:
            at, piece = at - plan[piece], piece + 1
        weight = SPRING * masses[:, here]
        other = short[piece][:, at * TILE : at * TILE + size] + every[seat(order, odd_ref[0], share)]
        for c in range(3):
            pull = last[c, :, here] + following[c, :, here] - 2.0 * pos[c, :, here]
            out_ref[c, :, here] = other[c : c + 1] + weight * pull


def total(order, plan, odd, *arrays):
    shapes = (arrays[0].shape, arrays[5].shape)
    return pl.pallas_call(
        functools.partial(total_kernel, order, plan),
        out_shape=[jax.ShapeDtypeStruct(shape, jnp.float32) for shape in shapes],
        in_specs=[pl.BlockSpec(memory_space=SMEM)]
        + [pl.BlockSpec(memory_space=VMEM)] * len(arrays),
        out_specs=[pl.BlockSpec(memory_space=VMEM)] * 2,
        compiler_params=pltpu.CompilerParams(vmem_limit_bytes=8 << 20),
        name="total",
    )(odd, *arrays)


def per_device(beads, spaces, positions, charges, polarizability, masses, neighbors):
    coords = positions.transpose(1, 0, 2)
    atom_dev = coords.shape[2]
    rim = HALO_T * TILE
    size = atom_dev // beads
    own_tiles = size // TILE
    assert size == rim
    across = math.gcd(beads, 8)
    bead = lax.axis_index("bead")

    def fold(b):
        row, at = b // across, b % across
        return row * across + (across - 1 - at if row % 2 else at)

    order = [fold(b) for b in range(beads)]
    row, at = bead // across, bead % across
    share = row * across + jnp.where(row % 2 == 1, across - 1 - at, at)
    odd = lax.axis_index("space") % 2
    share = jnp.where(odd == 1, beads - 1 - share, share)
    odd = odd.astype(jnp.int32).reshape(1)
    start = share * size

    def place(g):
        domain = g // beads
        return seat(order, domain % 2, g % beads) * spaces + domain

    count = beads * spaces
    fore = [(place(g), place((g + 1) % count)) for g in range(count)]
    back = [(j, i) for i, j in fore]
    home = [(place(g), (g % beads) * spaces + g // beads) for g in range(count)]
    both = ("bead", "space")

    def around(x):
        return lax.ppermute(x, both, fore), x, lax.ppermute(x, both, back)

    up = [(s, (s + 1) % spaces) for s in range(spaces)]
    down = [(j, i) for i, j in up]
    charges = charges[None]
    shares, first, final = pack(order, rim, odd, coords, charges)
    before = lax.ppermute(final, "space", up)
    after = lax.ppermute(first, "space", down)
    ext8 = extend(coords, before, after)
    near = jnp.concatenate([before[3:], charges, after[3:]], 1)
    near_charge = lax.dynamic_slice(near, (0, start), (1, size + 2 * rim))

    cent = jnp.sum(lax.all_to_all(shares, "bead", 0, 0), axis=0) / beads

    own_rows = lax.dynamic_slice(neighbors, (share * own_tiles, 0), (own_tiles, NBR))
    nb = own_rows - share * own_tiles
    alpha = lax.dynamic_slice(polarizability, (start,), (size,))[None]
    charge = lax.dynamic_slice(charges, (0, start), (1, size))

    tiles = atom_dev // TILE
    plan = [n * tiles // sum(PLAN) for n in PLAN]
    short = []

    def fill(after):
        first = sum(plan[: len(short)])
        short.append(short_range(ext8, neighbors.T, first, plan[len(short)], after))
        return short[-1]

    wait = fill(shares)
    cent, wait = lax.optimization_barrier((cent, wait))
    c3 = around(cent)
    wait = fill(cent)
    state, *weights = centre_first(nb, (wait,), *c3, near_charge, alpha)

    dip = state[:3]
    for _ in range(ITERS):
        d3 = around(dip)
        dip = centre_next(0, nb, (fill(dip),), *c3, *d3, alpha, state, *weights)
    d3 = around(dip)
    pulled = centre_next(beads, nb, (fill(dip),), *c3, *d3, charge, state, *weights)
    fill(pulled)
    every = lax.all_to_all(pulled, "bead", 0, 0)

    turn = [(b, (b + 1) % beads) for b in range(beads)]
    turn_back = [(j, i) for i, j in turn]
    late, pulled = lax.optimization_barrier((coords, pulled))
    last = lax.ppermute(late, "bead", turn)
    following = lax.ppermute(late, "bead", turn_back)
    dipoles = lax.ppermute(dip, both, home)
    forces, dipoles = total(
        order, plan, odd, coords, last, following, masses[None], every, dipoles, *short
    )
    return forces.transpose(1, 0, 2), dipoles


def solution(mesh):
    in_specs = (P("bead", None, "space"), P("space"), P("space"), P("space"), P("space", None))
    out_specs = (P("bead", None, "space"), P(None, ("space", "bead")))

    def body(*arrays):
        return per_device(mesh.shape["bead"], mesh.shape["space"], *arrays)

    return jax.shard_map(
        body, mesh=mesh, in_specs=in_specs, out_specs=out_specs, check_vma=False
    )
```
